32 devices in a mesh: sub: 8 (over z, y), grp: 4 (over x, core).
Axes of the slice: x: 2, y: 2, z: 4, core: 2. Of those that a mesh axis runs over, the one named last changes fastest.
Arguments:
- stiffness: bfloat16 [8, 64, 5, 256, 256], P('sub', 'grp'), may hold values from -0.0012207031 to 0.0012207031
- deflation: bfloat16 [8, 64, 16384], P('sub', None, 'grp'), may hold values from -6 to 6
- off_map: int32 [8, 3], replicated, may hold values from -2 to 2, as said below
- need_map: int32 [8, 4, 3, 4], P(None, 'grp'), may hold values from 0 to 15, as said below
- place_map: int32 [8, 4, 3, 4], P('sub', 'grp'), may hold values from 0 to 15, as said below
Outputs:
- coarse: float32 [8, 256, 256], P('sub', 'grp')
The draws below stay inside these ranges and needn't reach their ends.
Inputs may be any that keep to these rules, and one draw needn't show every extreme that they name: `off_map`: the 3 offsets of one row are distinct and nonzero. `need_map`: the 4 tile numbers of one row are distinct. `place_map`: the 4 tile numbers of one row are distinct.
All inputs are finite; a program needn't handle non-finite values.
Results may differ from the reference program's by a relative error of at most 0.0029.
Values may be sent and summed in bfloat16 or wider, within the bound.
A program may use at most 128 MiB of HBM per device.

```python
import jax
import jax.numpy as jnp
from jax import lax

TILE = 256
NVEC = 64
TD = 16
BAND = 5
NB = 3
RCH = 2
OV = 4
NBLK = 4
SUBS = 8
LAYERS = 4
ROWS_SUB = 16384


def pick_distinct(key, count, total, take):
    keys = jax.random.split(key, count)
    perms = jax.vmap(lambda one_key: jax.random.permutation(one_key, total))(keys)
    inner = 1 + jax.random.permutation(jax.random.fold_in(key, 5), total - 2)
    first = jnp.concatenate([jnp.array([0, total - 1], dtype=perms.dtype), inner.astype(perms.dtype)])
    return perms[:, :take].at[0].set(first[:take])


def draw_off_map(key, part):
    picks = pick_distinct(jax.random.fold_in(key, 17), SUBS, 2 * RCH, NB)
    return jnp.where(picks < RCH, picks - RCH, picks - RCH + 1).astype(jnp.int32)


def draw_need_map(key, part):
    picks = pick_distinct(jax.random.fold_in(key, 23), SUBS * LAYERS * NB, TD, OV)
    return picks.reshape(SUBS, LAYERS, NB, OV).astype(jnp.int32)


def draw_place_map(key, part):
    picks = pick_distinct(jax.random.fold_in(key, 29), SUBS * LAYERS * NB, TD, OV)
    return picks.reshape(SUBS, LAYERS, NB, OV).astype(jnp.int32)


def steps_of(stream_key, extent, cuts, least, top_value):
    factor_of, own = 1.0, jax.random.fold_in(stream_key, 6)
    for position, shards_of in cuts:
        steps = jnp.exp(jax.random.uniform(jax.random.fold_in(own, position), (shards_of,), jnp.float32, least / len(cuts), top_value / len(cuts)))
        factor_of = factor_of * jnp.repeat(steps, extent[position] // shards_of).reshape([-1 if axis == position else 1 for axis in range(len(extent))])
    return factor_of


def noise(own_key, dims, deviation, limit, cuts=(), kind=jnp.bfloat16):
    gain = steps_of(own_key, dims, cuts, -0.22, 0.18) if cuts else 1.0
    values = jax.random.normal(own_key, dims, jnp.float32) * deviation * gain
    return jnp.minimum(jnp.maximum(values, -limit), limit).astype(kind)


def setup_inputs(seed: int = 0) -> dict:
    streams_of = jax.random.split(jax.random.key(seed), 6)
    stiffness = noise(streams_of[0], (SUBS, LAYERS * TD, BAND, TILE, TILE), (BAND * TILE * ROWS_SUB) ** -0.5, 0.0012207031, ((0, 8), (1, 4)))
    deflation = noise(streams_of[1], (SUBS, NVEC, ROWS_SUB), 1.0, 6.0, ((0, 8), (2, 4)))
    off_map = draw_off_map(jax.random.fold_in(streams_of[5], 71), 0)
    need_map = draw_need_map(jax.random.fold_in(streams_of[5], 71), 0)
    place_map = draw_place_map(jax.random.fold_in(streams_of[5], 71), 0)
    return {"stiffness": stiffness, "deflation": deflation, "off_map": off_map, "need_map": need_map, "place_map": place_map}


def reference(stiffness, deflation, off_map, need_map, place_map):
    rim_tiles = BAND // 2
    all_tiles = LAYERS * TD
    basis_tiles = deflation.reshape(SUBS, NVEC, LAYERS, TD, TILE)
    layer_ids = jnp.arange(LAYERS, dtype=jnp.int32)[:, None]

    def subdomain_block(subdomain):
        own_basis = basis_tiles[subdomain]
        blocks = [own_basis]
        for slot_index in range(NB):
            other = jnp.mod(subdomain + off_map[subdomain, slot_index], SUBS).astype(jnp.int32)
            source = basis_tiles[other]
            needed = need_map[subdomain, :, slot_index, :]
            placed = place_map[subdomain, :, slot_index, :]
            picked = source[:, layer_ids, needed, :]
            blank_tiles = jnp.zeros_like(own_basis)
            blocks.append(blank_tiles.at[:, layer_ids, placed, :].set(picked))
        basis = jnp.concatenate(blocks, 0).reshape(NBLK * NVEC, all_tiles, TILE)
        padded = jnp.pad(basis, ((0, 0), (rim_tiles, rim_tiles), (0, 0))).astype(jnp.float32)
        local_stiffness = stiffness[subdomain]
        running = jnp.zeros((NBLK * NVEC, all_tiles, TILE), jnp.float32)
        for band_index in range(BAND):
            window = padded[:, band_index:band_index + all_tiles]
            tiles_now = local_stiffness[:, band_index].astype(jnp.float32)
            running = running + jnp.einsum("ctk,tjk->ctj", window, tiles_now)
        product_image = running.astype(jnp.bfloat16)
        flat_basis = basis.reshape(NBLK * NVEC, all_tiles * TILE)
        flat_image = product_image.reshape(NBLK * NVEC, all_tiles * TILE)
        return jnp.dot(flat_basis, flat_image.T, preferred_element_type=jnp.float32)

    return lax.map(subdomain_block, jnp.arange(SUBS, dtype=jnp.int32))
```

```python
import functools

import jax
import jax.numpy as jnp
from jax import lax
from jax.experimental import pallas as pl
from jax.experimental.pallas import tpu as pltpu
from jax.sharding import PartitionSpec as P

RCH = 2
MESH = pl.DeviceIdType.MESH
OFFSETS = [value for value in range(-RCH, RCH + 1) if value != 0]
NT = (((1,), (1,)), ((), ()))


def dot_nt(lhs, rhs):
    return lax.dot_general(lhs, rhs, NT, preferred_element_type=jnp.float32)


def kernel(
    subs, layers, off_ref, need_ref, place_ref, defl_ref, stiff_ref, out_ref,
    a_buf, basis, image, own_tiles, outgoing, arrived, part, part_low, shares,
    a_sem, sub_send, sub_recv, own_send, own_recv, rim_send, rim_recv, red_send, red_recv,
):
    s = lax.axis_index("sub")
    g = lax.axis_index("grp")
    _, tiles, bands, rows, _ = stiff_ref.shape
    vectors = defl_ref.shape[1]
    slots = off_ref.shape[0]
    overlap = place_ref.shape[3]
    rim = bands // 2
    halo = rim * rows
    width = tiles * rows
    columns = vectors * (slots + 1)
    share = out_ref.shape[1]
    has_left = g > 0
    has_right = g < layers - 1

    def stiff_copy(t):
        return pltpu.make_async_copy(stiff_ref.at[0, t], a_buf.at[t], a_sem.at[t])

    edge_low = list(range(rim))
    edge_high = list(range(tiles - rim, tiles))
    interior = list(range(rim, tiles - rim))

    barrier = pltpu.get_barrier_semaphore()
    for offset in OFFSETS:
        pl.semaphore_signal(
            barrier, inc=1, device_id=(lax.rem(s + offset + subs, subs), g), device_id_type=MESH
        )
    for step in range(1, layers):
        pl.semaphore_signal(
            barrier, inc=1, device_id=(s, lax.rem(g + step, layers)), device_id_type=MESH
        )
    for t in interior + edge_low + edge_high:
        stiff_copy(t).start()

    for u in range(tiles):
        own_tiles[u] = defl_ref[0, :, u * rows : (u + 1) * rows]
    for k, offset in enumerate(OFFSETS):
        target = lax.rem(s + offset + subs, subs)
        for o in range(overlap):
            tile = jnp.int32(0)
            for n in range(slots):
                match = (off_ref[n, target] == -offset).astype(jnp.int32)
                tile = tile + match * need_ref[0, n, o, target]
            outgoing[k, o] = own_tiles[tile]
    for k in range(len(OFFSETS)):
        arrived[k * (overlap + 1) + overlap] = jnp.zeros((vectors, rows), arrived.dtype)
    basis[0:vectors, halo : halo + width] = defl_ref[0]

    @pl.when(jnp.logical_not(has_left))
    def _():
        basis[:, 0:halo] = jnp.zeros((columns, halo), basis.dtype)

    @pl.when(jnp.logical_not(has_right))
    def _():
        basis[:, halo + width :] = jnp.zeros((columns, halo), basis.dtype)

    pl.semaphore_wait(barrier, len(OFFSETS) + layers - 1)

    count = len(OFFSETS)
    sub_copies = []
    for k, offset in enumerate(OFFSETS):
        sub_copies.append(
            pltpu.make_async_remote_copy(
                src_ref=outgoing.at[k],
                dst_ref=arrived.at[pl.ds((count - 1 - k) * (overlap + 1), overlap)],
                send_sem=sub_send.at[k],
                recv_sem=sub_recv.at[count - 1 - k],
                device_id=(lax.rem(s + offset + subs, subs), g),
                device_id_type=MESH,
            )
        )
    for copy in sub_copies:
        copy.start()

    def own_left():
        return pltpu.make_async_remote_copy(
            src_ref=defl_ref.at[0, :, pl.ds(0, halo)],
            dst_ref=basis.at[pl.ds(0, vectors), pl.ds(halo + width, halo)],
            send_sem=own_send.at[0],
            recv_sem=own_recv.at[1],
            device_id=(s, g - 1),
            device_id_type=MESH,
        )

    def own_right():
        return pltpu.make_async_remote_copy(
            src_ref=defl_ref.at[0, :, pl.ds(width - halo, halo)],
            dst_ref=basis.at[pl.ds(0, vectors), pl.ds(0, halo)],
            send_sem=own_send.at[1],
            recv_sem=own_recv.at[0],
            device_id=(s, g + 1),
            device_id_type=MESH,
        )

    def rim_left():
        return pltpu.make_async_remote_copy(
            src_ref=basis.at[pl.ds(vectors, columns - vectors), pl.ds(halo, halo)],
            dst_ref=basis.at[pl.ds(vectors, columns - vectors), pl.ds(halo + width, halo)],
            send_sem=rim_send.at[0],
            recv_sem=rim_recv.at[1],
            device_id=(s, g - 1),
            device_id_type=MESH,
        )

    def rim_right():
        return pltpu.make_async_remote_copy(
            src_ref=basis.at[pl.ds(vectors, columns - vectors), pl.ds(width, halo)],
            dst_ref=basis.at[pl.ds(vectors, columns - vectors), pl.ds(0, halo)],
            send_sem=rim_send.at[1],
            recv_sem=rim_recv.at[0],
            device_id=(s, g + 1),
            device_id_type=MESH,
        )

    def start_pair(left, right):
        @pl.when(has_left)
        def _():
            left().start()

        @pl.when(has_right)
        def _():
            right().start()

    def wait_pair(left, right):
        @pl.when(has_left)
        def _():
            right().wait_recv()
            left().wait_send()

        @pl.when(has_right)
        def _():
            left().wait_recv()
            right().wait_send()

    start_pair(own_left, own_right)

    def image_of(t, low, high):
        running = None
        for b in range(bands):
            start = (t + b) * rows
            if not isinstance(t, int):
                start = pl.multiple_of(start, rows)
            term = dot_nt(basis[low:high, pl.ds(start, rows)], a_buf[t, b])
            running = term if running is None else running + term
        at = t * rows if isinstance(t, int) else pl.multiple_of(t * rows, rows)
        image[low:high, pl.ds(at, rows)] = running.astype(image.dtype)

    def own_step(t, carry):
        stiff_copy(t).wait()
        image_of(t, 0, vectors)
        return carry

    lax.fori_loop(rim, tiles - rim, own_step, 0)
    wait_pair(own_left, own_right)
    for t in edge_low + edge_high:
        stiff_copy(t).wait()
        image_of(t, 0, vectors)

    for copy in sub_copies:
        copy.wait()

    def place(u, n):
        offset = off_ref[n, s]
        position = offset + RCH - (offset > 0).astype(jnp.int32)
        where_from = position * (overlap + 1) + overlap
        for o in range(overlap):
            hit = (place_ref[0, n, 0, o] == u).astype(jnp.int32)
            where_from = where_from + (o - overlap) * hit
        at = halo + u * rows
        if not isinstance(u, int):
            at = pl.multiple_of(at, rows)
        basis[(n + 1) * vectors : (n + 2) * vectors, pl.ds(at, rows)] = arrived[where_from]

    for u in edge_low + edge_high:
        for n in range(slots):
            place(u, n)

    def place_step(u, carry):
        for n in range(slots):
            place(u, n)
        return carry

    start_pair(rim_left, rim_right)
    lax.fori_loop(rim, tiles - rim, place_step, 0)

    def rest_step(t, carry):
        image_of(t, vectors, columns)
        return carry

    lax.fori_loop(rim, tiles - rim, rest_step, 0, unroll=2)
    inner = (tiles - 2 * rim) * rows
    part[...] = dot_nt(basis[:, 2 * halo : 2 * halo + inner], image[:, halo : halo + inner])

    wait_pair(rim_left, rim_right)
    for t in edge_low + edge_high:
        image_of(t, vectors, columns)
    total = part[...]
    total = total + dot_nt(basis[:, halo : 2 * halo], image[:, 0:halo])
    total = total + dot_nt(basis[:, width : width + halo], image[:, width - halo :])
    part[...] = total
    part_low[...] = total.astype(part_low.dtype)

    red_copies = []
    for step in range(1, layers):
        peer = lax.rem(g + step, layers)
        red_copies.append(
            pltpu.make_async_remote_copy(
                src_ref=part_low.at[pl.ds(pl.multiple_of(peer * share, share), share)],
                dst_ref=shares.at[step - 1],
                send_sem=red_send.at[step - 1],
                recv_sem=red_recv.at[step - 1],
                device_id=(s, peer),
                device_id_type=MESH,
            )
        )
    for copy in red_copies:
        copy.start()
    for copy in red_copies:
        copy.wait()
    result = part[pl.ds(pl.multiple_of(g * share, share), share), :]
    for step in range(1, layers):
        result = result + shares[step - 1].astype(jnp.float32)
    out_ref[0] = result


def on_device(subs, layers, stiffness, deflation, off_map, need_map, place_map):
    _, tiles, bands, rows, _ = stiffness.shape
    _, vectors, width = deflation.shape
    slots, overlap = place_map.shape[2:]
    columns = vectors * (slots + 1)
    halo = (bands // 2) * rows
    share = columns // layers
    count = len(OFFSETS)
    low = deflation.dtype
    dma = pltpu.SemaphoreType.DMA
    smem = pl.BlockSpec(memory_space=pltpu.SMEM)
    return pl.pallas_call(
        functools.partial(kernel, subs, layers),
        out_shape=jax.ShapeDtypeStruct((1, share, columns), jnp.float32),
        in_specs=[
            smem, smem, smem,
            pl.BlockSpec(memory_space=pltpu.VMEM),
            pl.BlockSpec(memory_space=pl.ANY),
        ],
        out_specs=pl.BlockSpec(memory_space=pltpu.VMEM),
        scratch_shapes=[
            pltpu.VMEM((tiles, bands, rows, rows), low),
            pltpu.VMEM((columns, width + 2 * halo), low),
            pltpu.VMEM((columns, width), low),
            pltpu.VMEM((tiles, vectors, rows), low),
            pltpu.VMEM((count, overlap, vectors, rows), low),
            pltpu.VMEM((count * (overlap + 1), vectors, rows), low),
            pltpu.VMEM((columns, columns), jnp.float32),
            pltpu.VMEM((columns, columns), low),
            pltpu.VMEM((layers - 1, share, columns), low),
            dma((tiles,)),
            dma((count,)), dma((count,)),
            dma((2,)), dma((2,)),
            dma((2,)), dma((2,)),
            dma((layers - 1,)), dma((layers - 1,)),
        ],
        compiler_params=pltpu.CompilerParams(collective_id=0, has_side_effects=True),
    )(
        off_map.T,
        need_map.transpose(1, 2, 3, 0),
        place_map.transpose(0, 2, 1, 3),
        deflation,
        stiffness,
    )


def solution(mesh):
    in_specs = (
        P("sub", "grp", None, None, None),
        P("sub", None, "grp"),
        P(),
        P(None, "grp", None, None),
        P("sub", "grp", None, None),
    )
    out_specs = P("sub", "grp", None)
    return jax.shard_map(
        functools.partial(on_device, mesh.shape["sub"], mesh.shape["grp"]),
        mesh=mesh,
        in_specs=in_specs,
        out_specs=out_specs,
        check_vma=False,
    )
```

```python
import functools

import jax
import jax.numpy as jnp
from jax import lax
from jax.experimental import pallas as pl
from jax.experimental.pallas import tpu as pltpu
from jax.sharding import PartitionSpec as P

RCH = 2
MESH = pl.DeviceIdType.MESH
OFFSETS = [value for value in range(-RCH, RCH + 1) if value != 0]
SEND_ORDER = sorted(OFFSETS, key=lambda value: (value < 0, abs(value)))
CHUNKS = 1
NT = (((1,), (1,)), ((), ()))


def dot_nt(lhs, rhs):
    return lax.dot_general(lhs, rhs, NT, preferred_element_type=jnp.float32)


def kernel(
    subs, layers, chunks, off_hbm, need_hbm, place_hbm, defl_ref, stiff_ref, out_ref,
    off_ref, need_ref, place_ref, a_buf, basis, image, own_tiles, outgoing, part, part_low, shares,
    in_sem, a_sem, sub_send, sub_recv, own_send, own_recv, rim_send, rim_recv, red_send, red_recv,
    *arrived,
):
    s = lax.axis_index("sub")
    g = lax.axis_index("grp")
    _, tiles, bands, rows, _ = stiff_ref.shape
    vectors = defl_ref.shape[1]
    slots = off_ref.shape[0]
    overlap = place_ref.shape[3]
    rim = bands // 2
    halo = rim * rows
    width = tiles * rows
    columns = vectors * (slots + 1)
    share = out_ref.shape[1]
    depth = vectors // chunks
    count = len(OFFSETS)
    has_left = g > 0
    has_right = g < layers - 1

    barrier = pltpu.get_barrier_semaphore()
    for offset in SEND_ORDER:
        pl.semaphore_signal(
            barrier, inc=1, device_id=(lax.rem(s + offset + subs, subs), g), device_id_type=MESH
        )
    for step in range(1, layers):
        pl.semaphore_signal(
            barrier, inc=1, device_id=(s, lax.rem(g + step, layers)), device_id_type=MESH
        )

    inputs = [
        pltpu.make_async_copy(off_hbm, off_ref, in_sem.at[0]),
        pltpu.make_async_copy(need_hbm, need_ref, in_sem.at[1]),
        pltpu.make_async_copy(place_hbm, place_ref, in_sem.at[2]),
        pltpu.make_async_copy(
            defl_ref.at[0], basis.at[0, :, pl.ds(halo, width)], in_sem.at[3]
        ),
    ]
    for copy in inputs:
        copy.start()

    def stiff_copy(t):
        return pltpu.make_async_copy(stiff_ref.at[0, t], a_buf.at[t], a_sem.at[t])

    edges = list(range(rim)) + list(range(tiles - rim, tiles))
    for t in list(range(rim, tiles - rim)) + edges:
        stiff_copy(t).start()

    for buffer in arrived:
        for k in range(count):
            buffer[k * (overlap + 1) + overlap] = jnp.zeros((depth, rows), buffer.dtype)

    @pl.when(jnp.logical_not(has_left))
    def _():
        basis[:, :, 0:halo] = jnp.zeros((slots + 1, vectors, halo), basis.dtype)

    @pl.when(jnp.logical_not(has_right))
    def _():
        basis[:, :, halo + width :] = jnp.zeros((slots + 1, vectors, halo), basis.dtype)

    for copy in inputs:
        copy.wait()
    for u in range(tiles):
        own_tiles[u] = basis[0, :, halo + u * rows : halo + (u + 1) * rows]
    for k, offset in enumerate(OFFSETS):
        target = lax.rem(s + offset + subs, subs)
        for o in range(overlap):
            tile = jnp.int32(0)
            for n in range(slots):
                match = (off_ref[n, target] == -offset).astype(jnp.int32)
                tile = tile + match * need_ref[0, n, o, target]
            outgoing[k, o] = own_tiles[tile]

    pl.semaphore_wait(barrier, count + layers - 1)

    def sub_copy(k, h):
        back = count - 1 - k
        return pltpu.make_async_remote_copy(
            src_ref=outgoing.at[k, :, pl.ds(h * depth, depth)],
            dst_ref=arrived[h].at[pl.ds(back * (overlap + 1), overlap)],
            send_sem=sub_send.at[h, k],
            recv_sem=sub_recv.at[h, back],
            device_id=(lax.rem(s + OFFSETS[k] + subs, subs), g),
            device_id_type=MESH,
        )

    for h in range(chunks):
        for offset in SEND_ORDER:
            sub_copy(OFFSETS.index(offset), h).start()

    def edge_copy(blocks, lines, to_left, send, recv):
        source, target = (halo, halo + width) if to_left else (width, 0)
        return pltpu.make_async_remote_copy(
            src_ref=basis.at[blocks, lines, pl.ds(source, halo)],
            dst_ref=basis.at[blocks, lines, pl.ds(target, halo)],
            send_sem=send.at[0 if to_left else 1],
            recv_sem=recv.at[1 if to_left else 0],
            device_id=(s, g - 1 if to_left else g + 1),
            device_id_type=MESH,
        )

    def own_copy(to_left):
        return edge_copy(pl.ds(0, 1), pl.ds(0, vectors), to_left, own_send, own_recv)

    def rim_copy(h):
        return lambda to_left: edge_copy(
            pl.ds(1, slots), pl.ds(h * depth, depth), to_left, rim_send.at[h], rim_recv.at[h]
        )

    def start_pair(make):
        @pl.when(has_left)
        def _():
            make(True).start()

        @pl.when(has_right)
        def _():
            make(False).start()

    def wait_pair(make):
        @pl.when(has_left)
        def _():
            make(False).wait_recv()
            make(True).wait_send()

        @pl.when(has_right)
        def _():
            make(True).wait_recv()
            make(False).wait_send()

    start_pair(own_copy)

    def column(t):
        return t * rows if isinstance(t, int) else pl.multiple_of(t * rows, rows)

    def image_of(t, blocks, lines):
        running = None
        for b in range(bands):
            window = basis[blocks, lines, pl.ds(column(t + b), rows)]
            shape = window.shape
            term = dot_nt(window.reshape(-1, rows), a_buf[t, b])
            running = term if running is None else running + term
        image[blocks, lines, pl.ds(column(t), rows)] = running.astype(image.dtype).reshape(shape)

    def own_step(t, carry):
        stiff_copy(t).wait()
        image_of(t, slice(0, 1), slice(0, vectors))
        return carry

    lax.fori_loop(rim, tiles - rim, own_step, 0, unroll=2)
    wait_pair(own_copy)
    for t in edges:
        stiff_copy(t).wait()
        image_of(t, slice(0, 1), slice(0, vectors))

    def place(h, u, n):
        offset = off_ref[n, s]
        position = offset + RCH - (offset > 0).astype(jnp.int32)
        found = position * (overlap + 1) + overlap
        for o in range(overlap):
            hit = (place_ref[0, n, 0, o] == u).astype(jnp.int32)
            found = found + (o - overlap) * hit
        lines = slice(h * depth, (h + 1) * depth)
        basis[n + 1, lines, pl.ds(halo + column(u), rows)] = arrived[h][found]

    for h in range(chunks):
        lines = slice(h * depth, (h + 1) * depth)
        for k in range(count):
            sub_copy(k, h).wait_recv()
        for u in edges:
            for n in range(slots):
                place(h, u, n)

        def place_step(u, carry):
            for n in range(slots):
                place(h, u, n)
            return carry

        lax.fori_loop(rim, tiles - rim, place_step, 0)
        start_pair(rim_copy(h))

        def rest_step(t, carry):
            image_of(t, slice(1, slots + 1), lines)
            return carry

        lax.fori_loop(rim, tiles - rim, rest_step, 0, unroll=2)
    for h in range(chunks):
        for k in range(count):
            sub_copy(k, h).wait_send()

    def partial(first, last):
        left = basis[:, :, halo + first * rows : halo + last * rows]
        right = image[:, :, first * rows : last * rows]
        return dot_nt(left.reshape(columns, -1), right.reshape(columns, -1))

    for h in range(chunks):
        if h == chunks - 1:
            part[...] = partial(rim, tiles - rim)
        wait_pair(rim_copy(h))
        for t in edges:
            image_of(t, slice(1, slots + 1), slice(h * depth, (h + 1) * depth))
    total = part[...] + partial(0, rim) + partial(tiles - rim, tiles)
    part_low[...] = total.astype(part_low.dtype)
    part[...] = total

    red_copies = []
    for step in range(1, layers):
        peer = lax.rem(g + step, layers)
        red_copies.append(
            pltpu.make_async_remote_copy(
                src_ref=part_low.at[pl.ds(pl.multiple_of(peer * share, share), share)],
                dst_ref=shares.at[step - 1],
                send_sem=red_send.at[step - 1],
                recv_sem=red_recv.at[step - 1],
                device_id=(s, peer),
                device_id_type=MESH,
            )
        )
    for copy in red_copies:
        copy.start()
    for copy in red_copies:
        copy.wait()
    result = part[pl.ds(pl.multiple_of(g * share, share), share), :]
    for step in range(1, layers):
        result = result + shares[step - 1].astype(jnp.float32)
    out_ref[0] = result


def on_device(subs, layers, stiffness, deflation, off_map, need_map, place_map):
    _, tiles, bands, rows, _ = stiffness.shape
    _, vectors, width = deflation.shape
    slots, overlap = place_map.shape[2:]
    columns = vectors * (slots + 1)
    halo = (bands // 2) * rows
    share = columns // layers
    count = len(OFFSETS)
    chunks = CHUNKS
    low = deflation.dtype
    dma = pltpu.SemaphoreType.DMA
    tables = (
        off_map.T,
        need_map.transpose(1, 2, 3, 0),
        place_map.transpose(0, 2, 1, 3),
    )
    return pl.pallas_call(
        functools.partial(kernel, subs, layers, chunks),
        out_shape=pltpu.VMEM((1, share, columns), jnp.float32),
        in_specs=[pl.BlockSpec(memory_space=pl.ANY)] * 5,
        out_specs=pl.BlockSpec(memory_space=pltpu.VMEM),
        scratch_shapes=[
            *[pltpu.SMEM(table.shape, table.dtype) for table in tables],
            pltpu.VMEM((tiles, bands, rows, rows), low),
            pltpu.VMEM((slots + 1, vectors, width + 2 * halo), low),
            pltpu.VMEM((slots + 1, vectors, width), low),
            pltpu.VMEM((tiles, vectors, rows), low),
            pltpu.VMEM((count, overlap, vectors, rows), low),
            pltpu.VMEM((columns, columns), jnp.float32),
            pltpu.VMEM((columns, columns), low),
            pltpu.VMEM((layers - 1, share, columns), low),
            dma((4,)),
            dma((tiles,)),
            dma((chunks, count)), dma((chunks, count)),
            dma((2,)), dma((2,)),
            dma((chunks, 2)), dma((chunks, 2)),
            dma((layers - 1,)), dma((layers - 1,)),
            *[pltpu.VMEM((count * (overlap + 1), vectors // chunks, rows), low)] * chunks,
        ],
        compiler_params=pltpu.CompilerParams(collective_id=0, has_side_effects=True),
    )(*tables, deflation, stiffness)


def solution(mesh):
    in_specs = (
        P("sub", "grp", None, None, None),
        P("sub", None, "grp"),
        P(),
        P(None, "grp", None, None),
        P("sub", "grp", None, None),
    )
    out_specs = P("sub", "grp", None)
    return jax.shard_map(
        functools.partial(on_device, mesh.shape["sub"], mesh.shape["grp"]),
        mesh=mesh,
        in_specs=in_specs,
        out_specs=out_specs,
        check_vma=False,
    )
```

```python
import functools

import jax
import jax.numpy as jnp
from jax import lax
from jax.experimental import pallas as pl
from jax.experimental.pallas import tpu as pltpu
from jax.sharding import PartitionSpec as P

RCH = 2
MESH = pl.DeviceIdType.MESH
OFFSETS = [value for value in range(-RCH, RCH + 1) if value != 0]
SEND_ORDER = sorted(OFFSETS, key=lambda value: (value < 0, abs(value)))
CHUNKS = 1
NT = (((1,), (1,)), ((), ()))


def dot_nt(lhs, rhs):
    return lax.dot_general(lhs, rhs, NT, preferred_element_type=jnp.float32)


def kernel(
    subs, layers, chunks, off_hbm, need_hbm, place_hbm, defl_ref, stiff_ref, out_ref,
    off_ref, need_ref, place_ref, a_buf, basis, image, own_tiles, outgoing, part, part_low, shares,
    in_sem, a_sem, sub_send, sub_recv, own_send, own_recv, rim_send, rim_recv, red_send, red_recv,
    *arrived,
):
    s = lax.axis_index("sub")
    g = lax.axis_index("grp")
    _, tiles, bands, rows, _ = stiff_ref.shape
    vectors = defl_ref.shape[1]
    slots = off_ref.shape[0]
    overlap = place_ref.shape[3]
    rim = bands // 2
    halo = rim * rows
    width = tiles * rows
    columns = vectors * (slots + 1)
    share = out_ref.shape[1]
    depth = vectors // chunks
    count = len(OFFSETS)
    has_left = g > 0
    has_right = g < layers - 1

    barrier = pltpu.get_barrier_semaphore()
    for offset in SEND_ORDER:
        pl.semaphore_signal(
            barrier, inc=1, device_id=(lax.rem(s + offset + subs, subs), g), device_id_type=MESH
        )
    for step in range(1, layers):
        pl.semaphore_signal(
            barrier, inc=1, device_id=(s, lax.rem(g + step, layers)), device_id_type=MESH
        )

    inputs = [
        pltpu.make_async_copy(off_hbm, off_ref, in_sem.at[0]),
        pltpu.make_async_copy(need_hbm, need_ref, in_sem.at[1]),
        pltpu.make_async_copy(place_hbm, place_ref, in_sem.at[2]),
        pltpu.make_async_copy(
            defl_ref.at[0], basis.at[0, :, pl.ds(halo, width)], in_sem.at[3]
        ),
    ]
    for copy in inputs:
        copy.start()

    def stiff_copy(t):
        return pltpu.make_async_copy(stiff_ref.at[0, t], a_buf.at[t], a_sem.at[t])

    edges = list(range(rim)) + list(range(tiles - rim, tiles))
    for t in list(range(rim, tiles - rim)) + edges:
        stiff_copy(t).start()

    for buffer in arrived:
        for k in range(count):
            buffer[k * (overlap + 1) + overlap] = jnp.zeros((depth, rows), buffer.dtype)

    @pl.when(jnp.logical_not(has_left))
    def _():
        basis[:, :, 0:halo] = jnp.zeros((slots + 1, vectors, halo), basis.dtype)

    @pl.when(jnp.logical_not(has_right))
    def _():
        basis[:, :, halo + width :] = jnp.zeros((slots + 1, vectors, halo), basis.dtype)

    for copy in inputs:
        copy.wait()
    for u in range(tiles):
        own_tiles[u] = basis[0, :, halo + u * rows : halo + (u + 1) * rows]
    for k, offset in enumerate(OFFSETS):
        target = lax.rem(s + offset + subs, subs)
        for o in range(overlap):
            tile = jnp.int32(0)
            for n in range(slots):
                match = (off_ref[n, target] == -offset).astype(jnp.int32)
                tile = tile + match * need_ref[0, n, o, target]
            outgoing[k, o] = own_tiles[tile]

    pl.semaphore_wait(barrier, count + layers - 1)

    def sub_copy(k, h):
        back = count - 1 - k
        return pltpu.make_async_remote_copy(
            src_ref=outgoing.at[k, :, pl.ds(h * depth, depth)],
            dst_ref=arrived[h].at[pl.ds(back * (overlap + 1), overlap)],
            send_sem=sub_send.at[h, k],
            recv_sem=sub_recv.at[h, back],
            device_id=(lax.rem(s + OFFSETS[k] + subs, subs), g),
            device_id_type=MESH,
        )

    for h in range(chunks):
        for offset in SEND_ORDER:
            sub_copy(OFFSETS.index(offset), h).start()

    def edge_copy(blocks, lines, to_left, send, recv):
        source, target = (halo, halo + width) if to_left else (width, 0)
        return pltpu.make_async_remote_copy(
            src_ref=basis.at[blocks, lines, pl.ds(source, halo)],
            dst_ref=basis.at[blocks, lines, pl.ds(target, halo)],
            send_sem=send.at[0 if to_left else 1],
            recv_sem=recv.at[1 if to_left else 0],
            device_id=(s, g - 1 if to_left else g + 1),
            device_id_type=MESH,
        )

    def own_copy(to_left):
        return edge_copy(pl.ds(0, 1), pl.ds(0, vectors), to_left, own_send, own_recv)

    def rim_copy(h):
        return lambda to_left: edge_copy(
            pl.ds(1, slots), pl.ds(h * depth, depth), to_left, rim_send.at[h], rim_recv.at[h]
        )

    def start_pair(make):
        @pl.when(has_left)
        def _():
            make(True).start()

        @pl.when(has_right)
        def _():
            make(False).start()

    def wait_pair(make):
        @pl.when(has_left)
        def _():
            make(False).wait_recv()
            make(True).wait_send()

        @pl.when(has_right)
        def _():
            make(True).wait_recv()
            make(False).wait_send()

    start_pair(own_copy)

    def column(t):
        return t * rows if isinstance(t, int) else pl.multiple_of(t * rows, rows)

    def image_of(t, blocks, lines):
        running = None
        for b in range(bands):
            window = basis[blocks, lines, pl.ds(column(t + b), rows)]
            shape = window.shape
            term = dot_nt(window.reshape(-1, rows), a_buf[t, b])
            running = term if running is None else running + term
        image[blocks, lines, pl.ds(column(t), rows)] = running.astype(image.dtype).reshape(shape)

    def own_step(t, carry):
        stiff_copy(t).wait()
        image_of(t, slice(0, 1), slice(0, vectors))
        return carry

    lax.fori_loop(rim, tiles - rim, own_step, 0, unroll=2)
    wait_pair(own_copy)
    for t in edges:
        stiff_copy(t).wait()
        image_of(t, slice(0, 1), slice(0, vectors))

    def place(h, u, n):
        offset = off_ref[n, s]
        position = offset + RCH - (offset > 0).astype(jnp.int32)
        found = position * (overlap + 1) + overlap
        for o in range(overlap):
            hit = (place_ref[0, n, 0, o] == u).astype(jnp.int32)
            found = found + (o - overlap) * hit
        lines = slice(h * depth, (h + 1) * depth)
        basis[n + 1, lines, pl.ds(halo + column(u), rows)] = arrived[h][found]

    for h in range(chunks):
        lines = slice(h * depth, (h + 1) * depth)
        for k in range(count):
            sub_copy(k, h).wait_recv()
        for u in edges:
            for n in range(slots):
                place(h, u, n)

        def place_step(u, carry):
            for n in range(slots):
                place(h, u, n)
            return carry

        lax.fori_loop(rim, tiles - rim, place_step, 0)
        start_pair(rim_copy(h))

        def rest_step(t, carry):
            image_of(t, slice(1, slots + 1), lines)
            return carry

        lax.fori_loop(rim, tiles - rim, rest_step, 0, unroll=tiles - 2 * rim)
    for h in range(chunks):
        for k in range(count):
            sub_copy(k, h).wait_send()

    def partial(first, last):
        left = basis[:, :, halo + first * rows : halo + last * rows]
        right = image[:, :, first * rows : last * rows]
        return dot_nt(left.reshape(columns, -1), right.reshape(columns, -1))

    for h in range(chunks):
        if h == chunks - 1:
            part[...] = partial(rim, tiles - rim)
        wait_pair(rim_copy(h))
        for t in edges:
            image_of(t, slice(1, slots + 1), slice(h * depth, (h + 1) * depth))
    total = part[...] + partial(0, rim) + partial(tiles - rim, tiles)
    part_low[...] = total.astype(part_low.dtype)
    part[...] = total

    red_copies = []
    for step in range(1, layers):
        peer = lax.rem(g + step, layers)
        red_copies.append(
            pltpu.make_async_remote_copy(
                src_ref=part_low.at[pl.ds(pl.multiple_of(peer * share, share), share)],
                dst_ref=shares.at[step - 1],
                send_sem=red_send.at[step - 1],
                recv_sem=red_recv.at[step - 1],
                device_id=(s, peer),
                device_id_type=MESH,
            )
        )
    for copy in red_copies:
        copy.start()
    for copy in red_copies:
        copy.wait()
    result = part[pl.ds(pl.multiple_of(g * share, share), share), :]
    for step in range(1, layers):
        result = result + shares[step - 1].astype(jnp.float32)
    out_ref[0] = result


def on_device(subs, layers, stiffness, deflation, off_map, need_map, place_map):
    _, tiles, bands, rows, _ = stiffness.shape
    _, vectors, width = deflation.shape
    slots, overlap = place_map.shape[2:]
    columns = vectors * (slots + 1)
    halo = (bands // 2) * rows
    share = columns // layers
    count = len(OFFSETS)
    chunks = CHUNKS
    low = deflation.dtype
    dma = pltpu.SemaphoreType.DMA
    tables = (
        off_map.T,
        need_map.transpose(1, 2, 3, 0),
        place_map.transpose(0, 2, 1, 3),
    )
    return pl.pallas_call(
        functools.partial(kernel, subs, layers, chunks),
        out_shape=pltpu.VMEM((1, share, columns), jnp.float32),
        in_specs=[pl.BlockSpec(memory_space=pl.ANY)] * 5,
        out_specs=pl.BlockSpec(memory_space=pltpu.VMEM),
        scratch_shapes=[
            *[pltpu.SMEM(table.shape, table.dtype) for table in tables],
            pltpu.VMEM((tiles, bands, rows, rows), low),
            pltpu.VMEM((slots + 1, vectors, width + 2 * halo), low),
            pltpu.VMEM((slots + 1, vectors, width), low),
            pltpu.VMEM((tiles, vectors, rows), low),
            pltpu.VMEM((count, overlap, vectors, rows), low),
            pltpu.VMEM((columns, columns), jnp.float32),
            pltpu.VMEM((columns, columns), low),
            pltpu.VMEM((layers - 1, share, columns), low),
            dma((4,)),
            dma((tiles,)),
            dma((chunks, count)), dma((chunks, count)),
            dma((2,)), dma((2,)),
            dma((chunks, 2)), dma((chunks, 2)),
            dma((layers - 1,)), dma((layers - 1,)),
            *[pltpu.VMEM((count * (overlap + 1), vectors // chunks, rows), low)] * chunks,
        ],
        compiler_params=pltpu.CompilerParams(collective_id=0, has_side_effects=True),
    )(*tables, deflation, stiffness)


def solution(mesh):
    in_specs = (
        P("sub", "grp", None, None, None),
        P("sub", None, "grp"),
        P(),
        P(None, "grp", None, None),
        P("sub", "grp", None, None),
    )
    out_specs = P("sub", "grp", None)
    return jax.shard_map(
        functools.partial(on_device, mesh.shape["sub"], mesh.shape["grp"]),
        mesh=mesh,
        in_specs=in_specs,
        out_specs=out_specs,
        check_vma=False,
    )
```
